32 devices in a mesh: expert: 4 (over y, core), dp: 8 (over z, x).
Axes of the slice: x: 2, y: 2, z: 4, core: 2. Of those that a mesh axis runs over, the one named last changes fastest.
Arguments:
- tokens: bfloat16 [4096, 1024], P(('expert', 'dp')), may hold values from -6 to 6
- d_output: bfloat16 [4096, 1024], P(('expert', 'dp')), may hold values from -6 to 6
- expert_ids: int32 [4096, 8], P(('expert', 'dp')), may hold values from 0 to 127, as said below
- gate_scores: bfloat16 [4096, 8], P(('expert', 'dp')), may hold values from 0.099609375 to 1
- gate_up_w: bfloat16 [4, 1024, 768], P('expert', 'dp'), may hold values from -0.1875 to 0.1875
- down_w: bfloat16 [4, 1024, 384], P('expert', 'dp'), may hold values from -0.3125 to 0.3125
Outputs:
- d_tokens: bfloat16 [4096, 1024], P(('expert', 'dp'))
- d_gates: bfloat16 [4096, 8], P(('expert', 'dp'))
- d_down: float32 [4, 1024, 384], P('expert', 'dp')
The draws below stay inside these ranges and needn't reach their ends.
Inputs may be any that keep to these rules, and one draw needn't show every extreme that they name: `expert_ids`: each token names 8 different experts. The tokens of one device name no expert more than 12 times, and in every draw one expert below 4 is named exactly 12 times by the tokens of every device.
All inputs are finite; a program needn't handle non-finite values.
Results may differ from the reference program's by a relative error of at most 0.0062.
Values may be sent and summed in bfloat16 or wider, within the bound.
A program may use at most 64 MiB of HBM per device.

```python
import math
import jax
import jax.numpy as jnp
from jax import lax

D = 1024
FF = 384
E_ALL = 128
TOPK = 8
TOK_DEV = 128
CAP = 12
EXPERTS = 4
TOKENS = 4096
N_EXPERT = 4
N_DP = 8


def draw_expert_ids(key, part):
    blocks = TOKENS // TOK_DEV
    mean_count = TOK_DEV * TOPK // E_ALL
    full_key, block_key = jax.random.split(jax.random.fold_in(key, 7311))
    heavy = jax.random.randint(full_key, (), 0, EXPERTS)
    block_keys = jax.random.split(block_key, blocks)

    def one_block(single_key):
        order_key, spread_key, column_key = jax.random.split(single_key, 3)
        order = jax.random.permutation(order_key, E_ALL).astype(jnp.int32)
        spread = jax.random.randint(spread_key, (E_ALL // 2,), 0, CAP - mean_count + 1)
        counts = jnp.zeros((E_ALL,), jnp.int32)
        counts = counts.at[order[0::2]].set(mean_count + spread)
        counts = counts.at[order[1::2]].set(mean_count - spread)
        position = jnp.sum(jnp.where(order == heavy, jnp.arange(E_ALL, dtype=jnp.int32), 0))
        partner = order[jnp.bitwise_xor(position, 1)]
        counts = counts.at[heavy].set(CAP).at[partner].set(2 * mean_count - CAP)
        running = jnp.cumsum(counts[order])
        places = jnp.arange(TOK_DEV * TOPK, dtype=jnp.int32)
        which = jnp.searchsorted(running, places, side='right').astype(jnp.int32)
        labels = order[which].reshape(TOPK, TOK_DEV)
        columns = jax.random.permutation(column_key, TOK_DEV)
        return labels.T[columns]
    return jax.vmap(one_block)(block_keys).reshape(TOKENS, TOPK).astype(jnp.int32)


def steps_of(stream_key, shape, cuts, low, top_value):
    factor_of, own = 1.0, jax.random.fold_in(stream_key, 6)
    for axis_at, shards_of in cuts:
        heights = jnp.exp(jax.random.uniform(jax.random.fold_in(own, axis_at), (shards_of,), jnp.float32, low / len(cuts), top_value / len(cuts)))
        factor_of = factor_of * jnp.repeat(heights, shape[axis_at] // shards_of).reshape([-1 if axis == axis_at else 1 for axis in range(len(shape))])
    return factor_of


def scatter_about(own_key, dims, scale, limit, cuts=(), kind=jnp.bfloat16):
    result = jax.random.normal(own_key, dims, jnp.float32) * scale
    if len(cuts) > 0:
        result = steps_of(own_key, dims, cuts, -0.22, 0.18) * result
    return jnp.clip(result, min=-limit, max=limit).astype(kind)


def setup_inputs(seed: int = 0) -> dict:
    key_list = jax.random.split(jax.random.key(seed), 7)
    return {
        "tokens": scatter_about(key_list[0], (TOKENS, D), 1.0, 6.0, ((0, 32),)),
        "d_output": scatter_about(key_list[1], (TOKENS, D), 1.0, 6.0, ((0, 32),)),
        "expert_ids": draw_expert_ids(jax.random.fold_in(key_list[6], 71), 0),
        "gate_scores": jnp.clip(jnp.exp(math.log(1.0) - 2.306499 * jax.random.uniform(key_list[3], (TOKENS, TOPK), jnp.float32) ** steps_of(key_list[3], (TOKENS, TOPK), ((0, 32),), -0.2, 0.2)), 0.099609375, 1.0).astype(jnp.bfloat16),
        "gate_up_w": scatter_about(key_list[4], (EXPERTS, D, 2 * FF), D ** -0.5, 0.1875, ((0, 4), (1, 8))),
        "down_w": scatter_about(key_list[5], (EXPERTS, D, FF), FF ** -0.5, 0.3125, ((0, 4), (1, 8))),
    }


def to_half(values):
    return lax.optimization_barrier(values.astype(jnp.bfloat16)).astype(jnp.float32)


def matmul(left, right):
    return jnp.dot(left, right, precision=lax.Precision.HIGHEST, preferred_element_type=jnp.float32)


def reference(tokens, d_output, expert_ids, gate_scores, gate_up_w, down_w):
    most_rows = CAP * N_EXPERT * N_DP
    total_tokens = tokens.shape[0]
    width = down_w.shape[2]

    def expert_step(carry, expert):
        grad_tokens, grad_gates = carry
        chosen = expert_ids == expert
        picked = jnp.any(chosen, axis=1)
        row_index = jnp.nonzero(picked, size=most_rows, fill_value=0)[0].astype(jnp.int32)
        alive = (jnp.arange(most_rows) < jnp.sum(picked.astype(jnp.int32))).astype(jnp.float32)
        chosen_rows = chosen[row_index]
        inputs = tokens[row_index].astype(jnp.float32)
        upstream = d_output[row_index].astype(jnp.float32)
        gate_rows = jnp.sum(jnp.where(chosen_rows, gate_scores[row_index].astype(jnp.float32), 0.0), axis=1) * alive
        weight_gu = gate_up_w[expert].astype(jnp.float32)
        weight_down = down_w[expert].astype(jnp.float32)
        pre_act = matmul(inputs, weight_gu)
        gate_part = pre_act[:, :width]
        up_part = pre_act[:, width:]
        sigma = jax.nn.sigmoid(gate_part)
        activ = gate_part * sigma
        hidden = to_half(activ * up_part)
        expert_out = matmul(hidden, weight_down.T)
        slot_grad = to_half(jnp.sum(upstream * expert_out, axis=1)) * alive
        d_expert_out = to_half(gate_rows[:, None] * upstream)
        d_hidden = matmul(d_expert_out, weight_down)
        d_gate_part = d_hidden * up_part * sigma * (1.0 + gate_part * (1.0 - sigma))
        d_up_part = d_hidden * activ
        d_pre = to_half(jnp.concatenate([d_gate_part, d_up_part], axis=1))
        d_slot = to_half(matmul(d_pre, weight_gu.T)) * alive[:, None]
        grad_down = matmul(d_expert_out.T, hidden)
        grad_tokens = grad_tokens.at[row_index].add(d_slot)
        grad_gates = grad_gates.at[row_index].add(jnp.where(chosen_rows, slot_grad[:, None], 0.0))
        return (grad_tokens, grad_gates), grad_down

    start = (jnp.zeros((total_tokens, tokens.shape[1]), jnp.float32), jnp.zeros(expert_ids.shape, jnp.float32))
    (grad_tokens, grad_gates), grad_down = lax.scan(expert_step, start, jnp.arange(EXPERTS, dtype=jnp.int32))
    return grad_tokens.astype(jnp.bfloat16), grad_gates.astype(jnp.bfloat16), grad_down
```

```python
import functools

import jax
import jax.numpy as jnp
from jax import lax
from jax.experimental import pallas as pl
from jax.experimental.pallas import tpu as pltpu
from jax.sharding import PartitionSpec as P

CAP = 12
PAD = 16
LANES = 128
BF = jnp.bfloat16
F32 = jnp.float32


def dot(left, right, dims=((1,), (0,))):
    return lax.dot_general(left, right, (dims, ((), ())), preferred_element_type=F32)


def kernel(groups, outer, inner, tok, dout, ids, scores, gate_in, down_in,
           o_tok, o_gates, o_down,
           gate_buf, down_buf, send, recv, hid_buf, dx_send, dx_buf, ret, back,
           w_send, w_recv, own_sem, s_send, s_recv, h_send, h_recv, x_send, x_recv, b_send, b_recv):
    n = outer * inner
    me = lax.axis_index("dp")
    mine = lax.axis_index("expert")
    zo = me // inner
    xi = me - zo * inner
    slots = groups * PAD
    rows = gate_in.shape[1]
    feats = tok.shape[1]
    width = down_in.shape[2]
    ins = (down_in, gate_in)
    bufs = (down_buf, gate_buf)

    barrier = pltpu.get_barrier_semaphore()
    for k in range(1, n):
        pl.semaphore_signal(barrier, inc=1, device_id={"dp": lax.rem(me + k, n)},
                            device_id_type=pl.DeviceIdType.MESH)
    for k in range(1, groups):
        pl.semaphore_signal(barrier, inc=1, device_id={"expert": lax.rem(mine + k, groups)},
                            device_id_type=pl.DeviceIdType.MESH)
    pl.semaphore_wait(barrier, n - 1 + groups - 1)

    def remote(src, dst, ss, rs, **where):
        return pltpu.make_async_remote_copy(
            src_ref=src, dst_ref=dst, send_sem=ss, recv_sem=rs,
            device_id=where, device_id_type=pl.DeviceIdType.MESH)

    def target(way):
        return me + (inner, -inner, 1, -1)[way]

    def can(way):
        return (zo < outer - 1, zo > 0, xi < inner - 1, xi > 0)[way]

    def hop(w, s, way, own=False):
        src = ins[w].at[0] if own else bufs[w].at[s]
        return remote(src, bufs[w].at[s], w_send.at[w, way, s], w_recv.at[w, s], dp=target(way))

    started = []

    def forward(s, way, valid, own=False):
        ok = can(way) if valid is None else jnp.logical_and(can(way), valid)

        @pl.when(ok)
        def _():
            for w in range(2):
                hop(w, s, way, own).start()
        started.append((ok, s, way, own))

    def arrive(s, valid):
        @pl.when(valid)
        def _():
            for w in range(2):
                hop(w, s, 0).wait_recv()

    for way in range(4):
        forward(me, way, None, own=True)
    own = [pltpu.make_async_copy(ins[w].at[0], bufs[w].at[me], own_sem.at[w]) for w in range(2)]
    for c in own:
        c.start()

    t_rows = tok.shape[0]
    topk = ids.shape[1]
    col = lax.broadcasted_iota(jnp.int32, (t_rows, slots), 1)
    col_e = col // PAD
    col_r = (col - col_e * PAD).astype(F32)
    idv = ids[...]
    scv = scores[...].astype(F32)
    live = jnp.zeros((t_rows, slots), F32)
    gcol = jnp.zeros((t_rows, slots), F32)
    hits = []
    for k in range(topk):
        hit = idv[:, k:k + 1] == col_e
        hits.append(hit)
        live = jnp.where(hit, 1.0, live)
        gcol = jnp.where(hit, scv[:, k:k + 1], gcol)
    lower = (lax.broadcasted_iota(jnp.int32, (t_rows, t_rows), 1)
             < lax.broadcasted_iota(jnp.int32, (t_rows, t_rows), 0))
    rank = dot(jnp.where(lower, 1.0, 0.0).astype(BF), live.astype(BF))
    pick = jnp.where(rank == col_r, live, 0.0)
    pick_t = jnp.transpose(pick).astype(BF)
    gate_t = jnp.transpose(pick * gcol)
    send[:, :feats] = dot(pick_t, tok[...]).astype(BF)
    send[:, feats:2 * feats] = dot(pick_t, dout[...]).astype(BF)
    send[:, 2 * feats:] = jnp.broadcast_to(
        jnp.sum(gate_t, axis=1, keepdims=True), (slots, LANES)).astype(BF)

    def block(e):
        return pl.ds(pl.multiple_of(e * PAD, PAD), PAD)

    def swap(src, dst, ss, rs, k):
        e = lax.rem(mine + k, groups)
        return remote(src.at[block(e), :], dst.at[block(mine), :], ss.at[k], rs.at[k], expert=e)

    for k in range(1, groups):
        swap(send, recv, s_send, s_recv, k).start()
    recv[block(mine), :] = send[block(mine), :]

    def peer(src, dst, ss, rs, k, sliced):
        d = lax.rem(me + k, n)
        return remote(src.at[d] if sliced else src.at[me], dst.at[me], ss.at[k], rs.at[k], dp=d)

    def outer_step(d):
        for way, s, valid in ((0, me - d * inner, zo >= d), (1, me + d * inner, zo + d < outer)):
            arrive(s, valid)
            for go in (way, 2, 3):
                forward(s, go, valid)

    outer_step(1) if outer > 1 else None

    for k in range(1, groups):
        swap(send, recv, s_send, s_recv, k).wait_recv()
    gates = recv[:, 2 * feats:2 * feats + 1].astype(F32)
    upstream = recv[:, feats:2 * feats]
    dexp = (gates * upstream.astype(F32)).astype(BF)
    for d in range(n):
        dx_send[d] = dexp[:, d * rows:(d + 1) * rows]
    for k in range(1, n):
        peer(dx_send, dx_buf, x_send, x_recv, k, True).start()
    dx_buf[me] = dx_send[me]

    for d in range(2, outer):
        outer_step(d)
    for di in range(1, inner):
        for d in range(outer):
            for sign in ((1,) if d == 0 else (-1, 1)):
                so = zo + sign * d
                good = jnp.logical_and(so >= 0, so < outer)
                for way, step in ((2, -di), (3, di)):
                    xs = xi + step
                    valid = jnp.logical_and(good, jnp.logical_and(xs >= 0, xs < inner))
                    s = so * inner + xs
                    arrive(s, valid)
                    if inner > 2:
                        forward(s, way, valid)
    for c in own:
        c.wait()

    gate_full = gate_buf[...].reshape(n * rows, 2 * width)
    down_full = down_buf[...].reshape(n * rows, width)
    u = dot(upstream, down_full)
    pre = dot(recv[:, :feats], gate_full)
    a = pre[:, :width]
    b = pre[:, width:]
    sig = jax.nn.sigmoid(a)
    act = a * sig
    hidden = (act * b).astype(BF)
    hid_buf[me] = hidden
    for k in range(1, n):
        peer(hid_buf, hid_buf, h_send, h_recv, k, False).start()
    d_hid = gates * u
    d_pre = jnp.concatenate(
        [d_hid * b * sig * (1.0 + a * (1.0 - sig)), d_hid * act], axis=1).astype(BF)
    ret[:, :feats] = dot(d_pre, gate_full, ((1,), (1,))).astype(BF)
    grad = jnp.sum(hidden.astype(F32) * u, axis=1, keepdims=True)
    ret[:, feats:] = jnp.broadcast_to(grad, (slots, LANES)).astype(BF)
    for k in range(1, groups):
        swap(ret, back, b_send, b_recv, k).start()
    back[block(mine), :] = ret[block(mine), :]

    for k in range(1, groups):
        swap(ret, back, b_send, b_recv, k).wait_recv()
    pick_b = pick.astype(BF)
    o_tok[...] = dot(pick_b, back[:, :feats]).astype(BF)
    slot_g = back[:, feats:]
    lane = lax.broadcasted_iota(jnp.int32, (t_rows, LANES), 1)
    total = jnp.zeros((t_rows, LANES), F32)
    for k in range(topk):
        got = dot(jnp.where(hits[k], pick, 0.0).astype(BF), slot_g)
        total = jnp.where(lane == k, got, total)
    o_gates[...] = total[:, :topk].astype(BF)

    o_down[0] = dot(dx_buf[me], hid_buf[me], ((0,), (0,)))
    for k in range(1, n):
        s = lax.rem(me - k + n, n)
        peer(dx_send, dx_buf, x_send, x_recv, k, True).wait_recv()
        peer(hid_buf, hid_buf, h_send, h_recv, k, False).wait_recv()
        o_down[0] += dot(dx_buf[s], hid_buf[s], ((0,), (0,)))

    for ok, s, way, is_own in started:
        @pl.when(ok)
        def _(s=s, way=way, is_own=is_own):
            for w in range(2):
                hop(w, s, way, is_own).wait_send()
    for k in range(1, groups):
        swap(send, recv, s_send, s_recv, k).wait_send()
        swap(ret, back, b_send, b_recv, k).wait_send()
    for k in range(1, n):
        peer(dx_send, dx_buf, x_send, x_recv, k, True).wait_send()
        peer(hid_buf, hid_buf, h_send, h_recv, k, False).wait_send()


def solution(mesh):
    groups = mesh.shape["expert"]
    n = mesh.shape["dp"]
    inner = 1
    while n % (inner * 2) == 0 and (inner * 2) ** 2 <= n:
        inner *= 2
    outer = n // inner

    def on_device(tokens, d_output, expert_ids, gate_scores, gate_up_w, down_w):
        feats = tokens.shape[1]
        rows = gate_up_w.shape[1]
        width = down_w.shape[2]
        slots = groups * PAD
        vmem = pl.BlockSpec(memory_space=pltpu.VMEM)
        dma = pltpu.SemaphoreType.DMA
        return pl.pallas_call(
            functools.partial(kernel, groups, outer, inner),
            out_shape=(
                jax.ShapeDtypeStruct(tokens.shape, BF),
                jax.ShapeDtypeStruct(gate_scores.shape, BF),
                jax.ShapeDtypeStruct(down_w.shape, F32),
            ),
            in_specs=[vmem] * 6,
            out_specs=(vmem,) * 3,
            scratch_shapes=[
                pltpu.VMEM((n, rows, 2 * width), BF),
                pltpu.VMEM((n, rows, width), BF),
                pltpu.VMEM((slots, 2 * feats + LANES), BF),
                pltpu.VMEM((slots, 2 * feats + LANES), BF),
                pltpu.VMEM((n, slots, width), BF),
                pltpu.VMEM((n, slots, rows), BF),
                pltpu.VMEM((n, slots, rows), BF),
                pltpu.VMEM((slots, feats + LANES), BF),
                pltpu.VMEM((slots, feats + LANES), BF),
                dma((2, 4, n)), dma((2, n)), dma((2,)),
                dma((groups,)), dma((groups,)),
                dma((n,)), dma((n,)),
                dma((n,)), dma((n,)),
                dma((groups,)), dma((groups,)),
            ],
            compiler_params=pltpu.CompilerParams(
                collective_id=0, has_side_effects=True, vmem_limit_bytes=60 * 2**20),
        )(tokens, d_output, expert_ids, gate_scores, gate_up_w, down_w)

    tok = P(("expert", "dp"), None)
    w = P("expert", "dp", None)
    return jax.shard_map(
        on_device, mesh=mesh, in_specs=(tok, tok, tok, tok, w, w),
        out_specs=(tok, tok, w), check_vma=False)
```

```python
import functools

import jax
import jax.numpy as jnp
from jax import lax
from jax.experimental import pallas as pl
from jax.experimental.pallas import tpu as pltpu
from jax.sharding import PartitionSpec as P

CAP = 12
PAD = 16
LANES = 128
BF = jnp.bfloat16
F32 = jnp.float32


def dot(left, right, dims=((1,), (0,))):
    return lax.dot_general(left, right, (dims, ((), ())), preferred_element_type=F32)


def kernel(groups, outer, inner, tok, dout, ids, scores, gate_in, down_in,
           o_tok, o_gates, o_down,
           gate_buf, down_buf, x_ch, up_ch, pre_acc, u_acc, send, recv, hid_buf, dx_send, dx_buf, ret, back,
           w_send, w_recv, own_sem, s_send, s_recv, h_send, h_recv, x_send, x_recv, b_send, b_recv):
    n = outer * inner
    me = lax.axis_index("dp")
    mine = lax.axis_index("expert")
    zo = me // inner
    xi = me - zo * inner
    slots = groups * PAD
    rows = gate_in.shape[1]
    feats = tok.shape[1]
    width = down_in.shape[2]
    ins = (down_in, gate_in)
    bufs = (down_buf, gate_buf)

    barrier = pltpu.get_barrier_semaphore()
    for k in range(1, n):
        pl.semaphore_signal(barrier, inc=1, device_id={"dp": lax.rem(me + k, n)},
                            device_id_type=pl.DeviceIdType.MESH)
    for k in range(1, groups):
        pl.semaphore_signal(barrier, inc=1, device_id={"expert": lax.rem(mine + k, groups)},
                            device_id_type=pl.DeviceIdType.MESH)
    pl.semaphore_wait(barrier, n - 1 + groups - 1)

    def remote(src, dst, ss, rs, **where):
        return pltpu.make_async_remote_copy(
            src_ref=src, dst_ref=dst, send_sem=ss, recv_sem=rs,
            device_id=where, device_id_type=pl.DeviceIdType.MESH)

    def target(way):
        return me + (inner, -inner, 1, -1)[way]

    def can(way):
        return (zo < outer - 1, zo > 0, xi < inner - 1, xi > 0)[way]

    def hop(w, s, way, own=False):
        src = ins[w].at[0] if own else bufs[w].at[s]
        return remote(src, bufs[w].at[s], w_send.at[w, way, s], w_recv.at[w, s], dp=target(way))

    started = []
    accs = (u_acc, pre_acc)
    chunks = (up_ch, x_ch)

    def forward(w, s, way, valid, own=False):
        ok = can(way) if valid is None else jnp.logical_and(can(way), valid)

        @pl.when(ok)
        def _():
            hop(w, s, way, own).start()
        started.append((ok, w, s, way, own))

    def arrive(w, s, valid):
        @pl.when(valid)
        def _():
            hop(w, s, 0).wait_recv()

    def add(w, s, valid):
        @pl.when(valid)
        def _():
            accs[w][...] += dot(chunks[w][s], bufs[w][s])

    def outer_shards(d):
        return ((0, me - d * inner, zo >= d), (1, me + d * inner, zo + d < outer))

    def outer_step(w, d):
        for way, s, valid in outer_shards(d):
            arrive(w, s, valid)
            for go in (way, 2, 3):
                forward(w, s, go, valid)

    def outer_add(w, d):
        for _, s, valid in outer_shards(d):
            add(w, s, valid)

    def inner_step(w, d):
        for di in range(1, inner):
            for sign in ((1,) if d == 0 else (-1, 1)):
                so = zo + sign * d
                good = jnp.logical_and(so >= 0, so < outer)
                for way, step in ((2, -di), (3, di)):
                    xs = xi + step
                    valid = jnp.logical_and(good, jnp.logical_and(xs >= 0, xs < inner))
                    s = so * inner + xs
                    arrive(w, s, valid)
                    if inner > 2:
                        forward(w, s, way, valid)
                    add(w, s, valid)

    own = [pltpu.make_async_copy(ins[w].at[0], bufs[w].at[me], own_sem.at[w]) for w in range(2)]
    for way in range(4):
        forward(1, me, way, None, own=True)
    for c in own:
        c.start()

    t_rows = tok.shape[0]
    topk = ids.shape[0]
    row = lax.broadcasted_iota(jnp.int32, (slots, t_rows), 0)
    row_e = row // PAD
    row_r = (row - row_e * PAD).astype(F32)
    idv = ids[...]
    scv = scores[...].astype(F32)
    live = jnp.zeros((slots, t_rows), F32)
    gcol = jnp.zeros((slots, t_rows), F32)
    hits = []
    for k in range(topk):
        hit = idv[k:k + 1, :] == row_e
        hits.append(hit)
        live = jnp.where(hit, 1.0, live)
        gcol = jnp.where(hit, scv[k:k + 1, :], gcol)
    upper = (lax.broadcasted_iota(jnp.int32, (t_rows, t_rows), 0)
             < lax.broadcasted_iota(jnp.int32, (t_rows, t_rows), 1))
    rank = dot(live.astype(BF), jnp.where(upper, 1.0, 0.0).astype(BF))
    pick_t = jnp.where(rank == row_r, live, 0.0)
    pick_b = pick_t.astype(BF)
    send[:, 2 * feats:] = jnp.broadcast_to(
        jnp.sum(pick_t * gcol, axis=1, keepdims=True), (slots, LANES)).astype(BF)
    send[:, :feats] = dot(pick_b, tok[...]).astype(BF)
    send[:, feats:2 * feats] = dot(pick_b, dout[...]).astype(BF)

    def block(e):
        return pl.ds(pl.multiple_of(e * PAD, PAD), PAD)

    def swap(src, dst, ss, rs, k):
        e = lax.rem(mine + k, groups)
        return remote(src.at[block(e), :], dst.at[block(mine), :], ss.at[k], rs.at[k], expert=e)

    for k in range(1, groups):
        swap(send, recv, s_send, s_recv, k).start()
    recv[block(mine), :] = send[block(mine), :]
    pick = jnp.transpose(pick_t).astype(BF)

    def peer(src, dst, ss, rs, k, sliced):
        d = lax.rem(me + k, n)
        return remote(src.at[d] if sliced else src.at[me], dst.at[me], ss.at[k], rs.at[k], dp=d)

    if outer > 1:
        outer_step(1, 1)

    packed = groups * CAP
    pr = lax.broadcasted_iota(jnp.int32, (packed, slots), 0)
    pc = lax.broadcasted_iota(jnp.int32, (packed, slots), 1)
    pack = jnp.where(pc == (pr // CAP) * PAD + pr % CAP, 1.0, 0.0).astype(BF)

    for k in range(1, groups):
        swap(send, recv, s_send, s_recv, k).wait_recv()
    gates = recv[:, 2 * feats:2 * feats + 1].astype(F32)
    upstream = recv[:, feats:2 * feats]
    dexp = dot(pack, (gates * upstream.astype(F32)).astype(BF)).astype(BF)
    for d in range(n):
        dx_send[d] = dexp[:, d * rows:(d + 1) * rows]
        x_ch[d] = recv[:, d * rows:(d + 1) * rows]
        up_ch[d] = recv[:, feats + d * rows:feats + (d + 1) * rows]
    for k in range(1, n):
        peer(dx_send, dx_buf, x_send, x_recv, k, True).start()
    dx_buf[me] = dx_send[me]
    pre_acc[...] = dot(x_ch[me], gate_in[0])
    u_acc[...] = dot(up_ch[me], down_in[0])

    for d in range(2, outer):
        outer_step(1, d)
        outer_add(1, d - 1)
    for way in range(2):
        forward(0, me, way, None, own=True)
    if outer > 1:
        outer_add(1, outer - 1)
    for d in range(outer):
        if d == outer - 1:
            for way in range(2, 4):
                forward(0, me, way, None, own=True)
            if outer > 1:
                outer_step(0, 1)
        inner_step(1, d)

    pre = pre_acc[...]
    a = pre[:, :width]
    b = pre[:, width:]
    sig = jax.nn.sigmoid(a)
    act = a * sig
    hidden = (act * b).astype(BF)
    hid_buf[me] = dot(pack, hidden).astype(BF)
    for k in range(1, n):
        peer(hid_buf, hid_buf, h_send, h_recv, k, False).start()

    for d in range(2, outer):
        outer_step(0, d)
    for d in range(1, outer):
        outer_add(0, d)
    for d in range(outer):
        inner_step(0, d)
    for c in own:
        c.wait()

    u = u_acc[...]
    d_hid = gates * u
    d_pre = jnp.concatenate(
        [d_hid * b * sig * (1.0 + a * (1.0 - sig)), d_hid * act], axis=1).astype(BF)
    gate_full = gate_buf[...].reshape(n * rows, 2 * width)
    ret[:, feats:] = jnp.broadcast_to(
        jnp.sum(hidden.astype(F32) * u, axis=1, keepdims=True), (slots, LANES)).astype(BF)
    ret[:, :feats] = dot(d_pre, gate_full, ((1,), (1,))).astype(BF)
    for k in range(1, groups):
        swap(ret, back, b_send, b_recv, k).start()
    back[block(mine), :] = ret[block(mine), :]

    o_down[0] = dot(dx_buf[me], hid_buf[me], ((0,), (0,)))
    for k in range(1, n):
        s = lax.rem(me - k + n, n)
        peer(dx_send, dx_buf, x_send, x_recv, k, True).wait_recv()
        peer(hid_buf, hid_buf, h_send, h_recv, k, False).wait_recv()
        o_down[0] += dot(dx_buf[s], hid_buf[s], ((0,), (0,)))

    for k in range(1, groups):
        swap(ret, back, b_send, b_recv, k).wait_recv()
    o_tok[...] = dot(pick, back[:, :feats]).astype(BF)
    weighted = pick_t * back[:, feats:feats + 1].astype(F32)
    o_gates[...] = jnp.concatenate(
        [jnp.sum(jnp.where(hit, weighted, 0.0), axis=0, keepdims=True) for hit in hits],
        axis=0).astype(BF)

    for ok, w, s, way, is_own in started:
        @pl.when(ok)
        def _(w=w, s=s, way=way, is_own=is_own):
            hop(w, s, way, is_own).wait_send()
    for k in range(1, groups):
        swap(send, recv, s_send, s_recv, k).wait_send()
        swap(ret, back, b_send, b_recv, k).wait_send()
    for k in range(1, n):
        peer(dx_send, dx_buf, x_send, x_recv, k, True).wait_send()
        peer(hid_buf, hid_buf, h_send, h_recv, k, False).wait_send()


def solution(mesh):
    groups = mesh.shape["expert"]
    n = mesh.shape["dp"]
    inner = 1
    while n % (inner * 2) == 0 and (inner * 2) ** 2 <= n:
        inner *= 2
    outer = n // inner

    def on_device(tokens, d_output, expert_ids, gate_scores, gate_up_w, down_w):
        feats = tokens.shape[1]
        rows = gate_up_w.shape[1]
        width = down_w.shape[2]
        slots = groups * PAD
        packed = groups * CAP
        vmem = pl.BlockSpec(memory_space=pltpu.VMEM)
        dma = pltpu.SemaphoreType.DMA
        grads, d_gates, d_down = pl.pallas_call(
            functools.partial(kernel, groups, outer, inner),
            out_shape=(
                jax.ShapeDtypeStruct(tokens.shape, BF),
                jax.ShapeDtypeStruct(gate_scores.shape[::-1], BF),
                jax.ShapeDtypeStruct(down_w.shape, F32),
            ),
            in_specs=[vmem] * 6,
            out_specs=(vmem,) * 3,
            scratch_shapes=[
                pltpu.VMEM((n, rows, 2 * width), BF),
                pltpu.VMEM((n, rows, width), BF),
                pltpu.VMEM((n, slots, rows), BF),
                pltpu.VMEM((n, slots, rows), BF),
                pltpu.VMEM((slots, 2 * width), F32),
                pltpu.VMEM((slots, width), F32),
                pltpu.VMEM((slots, 2 * feats + LANES), BF),
                pltpu.VMEM((slots, 2 * feats + LANES), BF),
                pltpu.VMEM((n, packed, width), BF),
                pltpu.VMEM((n, packed, rows), BF),
                pltpu.VMEM((n, packed, rows), BF),
                pltpu.VMEM((slots, feats + LANES), BF),
                pltpu.VMEM((slots, feats + LANES), BF),
                dma((2, 4, n)), dma((2, n)), dma((2,)),
                dma((groups,)), dma((groups,)),
                dma((n,)), dma((n,)),
                dma((n,)), dma((n,)),
                dma((groups,)), dma((groups,)),
            ],
            compiler_params=pltpu.CompilerParams(
                collective_id=0, has_side_effects=True, vmem_limit_bytes=60 * 2**20),
        )(tokens, d_output, expert_ids.T, gate_scores.T, gate_up_w, down_w)
        return grads, d_gates.T, d_down

    tok = P(("expert", "dp"), None)
    w = P("expert", "dp", None)
    return jax.shard_map(
        on_device, mesh=mesh, in_specs=(tok, tok, tok, tok, w, w),
        out_specs=(tok, tok, w), check_vma=False)
```

```python
import functools

import jax
import jax.numpy as jnp
from jax import lax
from jax.experimental import pallas as pl
from jax.experimental.pallas import tpu as pltpu
from jax.sharding import PartitionSpec as P

CAP = 12
PAD = 16
LANES = 128
BF = jnp.bfloat16
F32 = jnp.float32


def dot(left, right, dims=((1,), (0,))):
    return lax.dot_general(left, right, (dims, ((), ())), preferred_element_type=F32)


def kernel(groups, outer, inner, tok, dout, ids, scores, gate_in, down_in,
           o_tok, o_gates, o_down,
           gate_buf, down_buf, x_ch, up_ch, pre_acc, u_acc, send, recv, hid_buf, dx_send, dx_buf, ret, back,
           w_send, w_recv, own_sem, s_send, s_recv, h_send, h_recv, x_send, x_recv, b_send, b_recv):
    n = outer * inner
    me = lax.axis_index("dp")
    mine = lax.axis_index("expert")
    zo = me // inner
    xi = me - zo * inner
    slots = groups * PAD
    rows = gate_in.shape[1]
    feats = tok.shape[1]
    width = down_in.shape[2]
    ins = (down_in, gate_in)
    bufs = (down_buf, gate_buf)

    barrier = pltpu.get_barrier_semaphore()
    for k in range(1, n):
        pl.semaphore_signal(barrier, inc=1, device_id={"dp": lax.rem(me + k, n)},
                            device_id_type=pl.DeviceIdType.MESH)
    for k in range(1, groups):
        pl.semaphore_signal(barrier, inc=1, device_id={"expert": lax.rem(mine + k, groups)},
                            device_id_type=pl.DeviceIdType.MESH)
    pl.semaphore_wait(barrier, n - 1 + groups - 1)

    def remote(src, dst, ss, rs, **where):
        return pltpu.make_async_remote_copy(
            src_ref=src, dst_ref=dst, send_sem=ss, recv_sem=rs,
            device_id=where, device_id_type=pl.DeviceIdType.MESH)

    def target(way):
        return me + (inner, -inner, 1, -1)[way]

    def can(way):
        return (zo < outer - 1, zo > 0, xi < inner - 1, xi > 0)[way]

    def hop(w, s, way, own=False):
        src = ins[w].at[0] if own else bufs[w].at[s]
        return remote(src, bufs[w].at[s], w_send.at[w, way, s], w_recv.at[w, s], dp=target(way))

    started = []
    accs = (u_acc, pre_acc)
    chunks = (up_ch, x_ch)

    def forward(w, s, way, valid, own=False):
        ok = can(way) if valid is None else jnp.logical_and(can(way), valid)

        @pl.when(ok)
        def _():
            hop(w, s, way, own).start()
        started.append((ok, w, s, way, own))

    def arrive(w, s, valid):
        @pl.when(valid)
        def _():
            hop(w, s, 0).wait_recv()

    def add(w, s, valid):
        @pl.when(valid)
        def _():
            accs[w][...] += dot(chunks[w][s], bufs[w][s])

    def outer_shards(d):
        return ((0, me - d * inner, zo >= d), (1, me + d * inner, zo + d < outer))

    def outer_step(w, d):
        for way, s, valid in outer_shards(d):
            arrive(w, s, valid)
            for go in (way, 2, 3):
                forward(w, s, go, valid)

    def outer_add(w, d):
        for _, s, valid in outer_shards(d):
            add(w, s, valid)

    def inner_step(w, d):
        for di in range(1, inner):
            for sign in ((1,) if d == 0 else (-1, 1)):
                so = zo + sign * d
                good = jnp.logical_and(so >= 0, so < outer)
                for way, step in ((2, -di), (3, di)):
                    xs = xi + step
                    valid = jnp.logical_and(good, jnp.logical_and(xs >= 0, xs < inner))
                    s = so * inner + xs
                    arrive(w, s, valid)
                    if inner > 2:
                        forward(w, s, way, valid)
                    add(w, s, valid)

    own = [pltpu.make_async_copy(ins[w].at[0], bufs[w].at[me], own_sem.at[w]) for w in range(2)]
    for way in range(4):
        forward(1, me, way, None, own=True)
    for way in range(4):
        forward(0, me, way, None, own=True)
    for c in own:
        c.start()

    t_rows = tok.shape[0]
    topk = ids.shape[0]
    row = lax.broadcasted_iota(jnp.int32, (slots, t_rows), 0)
    row_e = row // PAD
    row_r = (row - row_e * PAD).astype(F32)
    idv = ids[...]
    scv = scores[...].astype(F32)
    live = jnp.zeros((slots, t_rows), F32)
    gcol = jnp.zeros((slots, t_rows), F32)
    hits = []
    for k in range(topk):
        hit = idv[k:k + 1, :] == row_e
        hits.append(hit)
        live = jnp.where(hit, 1.0, live)
        gcol = jnp.where(hit, scv[k:k + 1, :], gcol)
    upper = (lax.broadcasted_iota(jnp.int32, (t_rows, t_rows), 0)
             < lax.broadcasted_iota(jnp.int32, (t_rows, t_rows), 1))
    rank = dot(live.astype(BF), jnp.where(upper, 1.0, 0.0).astype(BF))
    pick_t = jnp.where(rank == row_r, live, 0.0)
    pick_b = pick_t.astype(BF)
    send[:, 2 * feats:] = jnp.broadcast_to(
        jnp.sum(pick_t * gcol, axis=1, keepdims=True), (slots, LANES)).astype(BF)
    send[:, :feats] = dot(pick_b, tok[...]).astype(BF)
    send[:, feats:2 * feats] = dot(pick_b, dout[...]).astype(BF)

    def block(e):
        return pl.ds(pl.multiple_of(e * PAD, PAD), PAD)

    def swap(src, dst, ss, rs, k):
        e = lax.rem(mine + k, groups)
        return remote(src.at[block(e), :], dst.at[block(mine), :], ss.at[k], rs.at[k], expert=e)

    for k in range(1, groups):
        swap(send, recv, s_send, s_recv, k).start()
    recv[block(mine), :] = send[block(mine), :]
    pick = jnp.transpose(pick_t).astype(BF)

    def peer(src, dst, ss, rs, k, sliced):
        d = lax.rem(me + k, n)
        return remote(src.at[d] if sliced else src.at[me], dst.at[me], ss.at[k], rs.at[k], dp=d)

    if outer > 1:
        outer_step(1, 1)
        outer_step(0, 1)

    packed = groups * CAP
    pr = lax.broadcasted_iota(jnp.int32, (packed, slots), 0)
    pc = lax.broadcasted_iota(jnp.int32, (packed, slots), 1)
    pack = jnp.where(pc == (pr // CAP) * PAD + pr % CAP, 1.0, 0.0).astype(BF)

    for k in range(1, groups):
        swap(send, recv, s_send, s_recv, k).wait_recv()
    gates = recv[:, 2 * feats:2 * feats + 1].astype(F32)
    upstream = recv[:, feats:2 * feats]
    dexp = dot(pack, (gates * upstream.astype(F32)).astype(BF)).astype(BF)
    for d in range(n):
        dx_send[d] = dexp[:, d * rows:(d + 1) * rows]
        x_ch[d] = recv[:, d * rows:(d + 1) * rows]
        up_ch[d] = recv[:, feats + d * rows:feats + (d + 1) * rows]
    for k in range(1, n):
        peer(dx_send, dx_buf, x_send, x_recv, k, True).start()
    dx_buf[me] = dx_send[me]
    pre_acc[...] = dot(x_ch[me], gate_in[0])
    u_acc[...] = dot(up_ch[me], down_in[0])

    for d in range(2, outer):
        outer_step(1, d)
        outer_step(0, d)
        outer_add(1, d - 1)
        outer_add(0, d - 1)
    for d in range(outer - 1):
        inner_step(1, d)
        inner_step(0, d)
    if outer > 1:
        outer_add(1, outer - 1)
        outer_add(0, outer - 1)
    inner_step(1, outer - 1)

    pre = pre_acc[...]
    a = pre[:, :width]
    b = pre[:, width:]
    sig = jax.nn.sigmoid(a)
    act = a * sig
    hidden = (act * b).astype(BF)
    hid_buf[me] = dot(pack, hidden).astype(BF)
    for k in range(1, n):
        peer(hid_buf, hid_buf, h_send, h_recv, k, False).start()

    inner_step(0, outer - 1)
    for c in own:
        c.wait()

    u = u_acc[...]
    d_hid = gates * u
    d_pre = jnp.concatenate(
        [d_hid * b * sig * (1.0 + a * (1.0 - sig)), d_hid * act], axis=1).astype(BF)
    gate_full = gate_buf[...].reshape(n * rows, 2 * width)
    ret[:, feats:] = jnp.broadcast_to(
        jnp.sum(hidden.astype(F32) * u, axis=1, keepdims=True), (slots, LANES)).astype(BF)
    ret[:, :feats] = dot(d_pre, gate_full, ((1,), (1,))).astype(BF)
    for k in range(1, groups):
        swap(ret, back, b_send, b_recv, k).start()
    back[block(mine), :] = ret[block(mine), :]

    o_down[0] = dot(dx_buf[me], hid_buf[me], ((0,), (0,)))
    for k in range(1, n):
        s = lax.rem(me - k + n, n)
        peer(dx_send, dx_buf, x_send, x_recv, k, True).wait_recv()
        peer(hid_buf, hid_buf, h_send, h_recv, k, False).wait_recv()
        o_down[0] += dot(dx_buf[s], hid_buf[s], ((0,), (0,)))

    for k in range(1, groups):
        swap(ret, back, b_send, b_recv, k).wait_recv()
    o_tok[...] = dot(pick, back[:, :feats]).astype(BF)
    weighted = pick_t * back[:, feats:feats + 1].astype(F32)
    o_gates[...] = jnp.concatenate(
        [jnp.sum(jnp.where(hit, weighted, 0.0), axis=0, keepdims=True) for hit in hits],
        axis=0).astype(BF)

    for ok, w, s, way, is_own in started:
        @pl.when(ok)
        def _(w=w, s=s, way=way, is_own=is_own):
            hop(w, s, way, is_own).wait_send()
    for k in range(1, groups):
        swap(send, recv, s_send, s_recv, k).wait_send()
        swap(ret, back, b_send, b_recv, k).wait_send()
    for k in range(1, n):
        peer(dx_send, dx_buf, x_send, x_recv, k, True).wait_send()
        peer(hid_buf, hid_buf, h_send, h_recv, k, False).wait_send()


def place(*refs):
    for src, dst in zip(refs[:3], refs[3:]):
        dst[...] = src[...]


def solution(mesh):
    groups = mesh.shape["expert"]
    n = mesh.shape["dp"]
    inner = 1
    while n % (inner * 2) == 0 and (inner * 2) ** 2 <= n:
        inner *= 2
    outer = n // inner

    def on_device(tokens, d_output, expert_ids, gate_scores, gate_up_w, down_w):
        feats = tokens.shape[1]
        rows = gate_up_w.shape[1]
        width = down_w.shape[2]
        slots = groups * PAD
        packed = groups * CAP
        vmem = pl.BlockSpec(memory_space=pltpu.VMEM)
        dma = pltpu.SemaphoreType.DMA
        grads, d_gates, d_down = pl.pallas_call(
            functools.partial(kernel, groups, outer, inner),
            out_shape=(
                jax.ShapeDtypeStruct(tokens.shape, BF),
                jax.ShapeDtypeStruct(gate_scores.shape[::-1], BF),
                jax.ShapeDtypeStruct(down_w.shape, F32),
            ),
            in_specs=[vmem] * 6,
            out_specs=(vmem,) * 3,
            scratch_shapes=[
                pltpu.VMEM((n, rows, 2 * width), BF),
                pltpu.VMEM((n, rows, width), BF),
                pltpu.VMEM((n, slots, rows), BF),
                pltpu.VMEM((n, slots, rows), BF),
                pltpu.VMEM((slots, 2 * width), F32),
                pltpu.VMEM((slots, width), F32),
                pltpu.VMEM((slots, 2 * feats + LANES), BF),
                pltpu.VMEM((slots, 2 * feats + LANES), BF),
                pltpu.VMEM((n, packed, width), BF),
                pltpu.VMEM((n, packed, rows), BF),
                pltpu.VMEM((n, packed, rows), BF),
                pltpu.VMEM((slots, feats + LANES), BF),
                pltpu.VMEM((slots, feats + LANES), BF),
                dma((2, 4, n)), dma((2, n)), dma((2,)),
                dma((groups,)), dma((groups,)),
                dma((n,)), dma((n,)),
                dma((n,)), dma((n,)),
                dma((groups,)), dma((groups,)),
            ],
            compiler_params=pltpu.CompilerParams(
                collective_id=0, has_side_effects=True, vmem_limit_bytes=60 * 2**20),
        )(tokens, d_output, expert_ids.T, gate_scores.T, gate_up_w, down_w)
        grads, d_gates, d_down = pl.pallas_call(
            place,
            out_shape=tuple(jax.ShapeDtypeStruct(v.shape, v.dtype) for v in (grads, d_gates, d_down)),
            in_specs=[vmem] * 3,
            out_specs=(vmem,) * 3,
        )(grads, d_gates, d_down)
        return grads, d_gates.T, d_down

    tok = P(("expert", "dp"), None)
    w = P("expert", "dp", None)
    return jax.shard_map(
        on_device, mesh=mesh, in_specs=(tok, tok, tok, tok, w, w),
        out_specs=(tok, tok, w), check_vma=False)
```
